128 devices in a mesh: row: 8 (over x_hi, z), col: 16 (over y, x_lo, core).
Axes of the slice: x: 4 (x_hi: 2, x_lo: 2; x = x_hi * 2 + x_lo), y: 4, z: 4, core: 2. Of those that a mesh axis runs over, the one named last changes fastest.
Arguments:
- positions: float32 [1024, 24576], P('row', 'col'), may hold values from -2.5 to 2.5
- momenta: float32 [1024, 24576], P('row', 'col'), may hold values from -2.5 to 2.5
- couplings: float32 [24576, 24576], P('row', 'col'), may hold values from -0.0390625 to 0.0390625
Outputs:
- positions_next: float32 [1024, 24576], P('row', 'col')
- momenta_next: float32 [1024, 24576], P('row', 'col')
The draws below stay inside these ranges and needn't reach their ends.
All inputs are finite; a program needn't handle non-finite values.
Results may differ from the reference program's by a relative error of at most 0.00005.
Values sent between devices are 32-bit elements; how exact they have to be, the bound alone decides.
A program may use at most 128 MiB of HBM per device.

```python
import jax
import jax.numpy as jnp
from jax import lax

N = 24576
R = 1024


def block_levels(own_key, extent, pieces, smallest, largest):
    def one(position, blocks):
        draws = jax.random.uniform(jax.random.fold_in(jax.random.fold_in(own_key, 6), position), (blocks,), jnp.float32, smallest / len(pieces), largest / len(pieces))
        return jnp.repeat(jnp.exp(draws), extent[position] // blocks).reshape((-1,) + (1,) * (len(extent) - position - 1))

    factor_of = one(*pieces[0])
    for cut in pieces[1:]:
        factor_of = factor_of * one(*cut)
    return factor_of


def normal_values(own_key, extent, deviation, bound, pieces=(), kind=jnp.bfloat16):
    array = deviation * jax.random.normal(own_key, extent, jnp.float32)
    if pieces:
        array = array * block_levels(own_key, extent, pieces, -0.22, 0.18)
    return jnp.clip(array, -bound, bound).astype(kind)


def setup_inputs(seed: int = 0) -> dict:
    arg_keys = jax.random.split(jax.random.key(seed), 4)
    positions = normal_values(arg_keys[0], (R, N), 0.4, 2.5, ((0, 8), (1, 16)), jnp.float32)
    momenta = normal_values(arg_keys[1], (R, N), 0.4, 2.5, ((0, 8), (1, 16)), jnp.float32)
    couplings = normal_values(arg_keys[2], (N, N), N ** -0.5, 0.0390625, ((0, 8), (1, 16)), jnp.float32)
    return dict(positions=positions, momenta=momenta, couplings=couplings)


time_step = 0.5
kerr_rate = 1.0
pump_rate = 0.6
detuning = 0.4
coupling_gain = 1.5


def reference(positions, momenta, couplings):
    coupled = jnp.dot(positions, couplings, precision=lax.Precision.HIGHEST, preferred_element_type=jnp.float32)
    radius = positions * positions + momenta * momenta
    momenta_next = momenta + time_step * (-(kerr_rate * radius - pump_rate + detuning) * positions + coupling_gain * coupled)
    radius_next = positions * positions + momenta_next * momenta_next
    positions_next = positions + time_step * (kerr_rate * radius_next + pump_rate + detuning) * momenta_next
    return positions_next, momenta_next
```

```python
import jax
import jax.numpy as jnp
from jax import lax
from jax.experimental import pallas as pl
from jax.experimental.pallas import tpu as pltpu
from jax.sharding import PartitionSpec as P

time_step = 0.5
kerr_rate = 1.0
pump_rate = 0.6
detuning = 0.4
coupling_gain = 1.5

MESH = pl.DeviceIdType.MESH
BF16 = jnp.bfloat16
F32 = jnp.float32
CHUNKS = 8
PIECE = 384
TILE = 512
(T, XL, UP, UP2, DN, DN2, UPR, DNR, SWAP, ZP, ZM, FP0, FP1, FM0, FM1, XH) = range(16)


def slot_of(a, b):
    xh, z = a // 4, a % 4
    y, xl = b // 2, b % 2
    return 2 * ((z + 2 * y + xl) % 4) + (xh + z // 2) % 2


def kernel(
    pos, coup, out, xg, jhi, jlo, stage, x2, p, rzp, rzm, rfp, rfm, rx, send, recv, stage_sem
):
    n, _, _, m, width = xg.shape
    row, col = lax.axis_index("row"), lax.axis_index("col")
    xh, z = row // 4, row % 4
    core = col % 2
    slot = col // 2
    y, xl = slot // 2, slot % 2
    up, down = (y + 1) % 4, (y + 3) % 4
    zup, zdown, zfar = (z + 1) % 4, (z + 3) % 4, (z + 2) % 4

    def at(row_, y_, xl_, core_):
        return {"row": row_, "col": (2 * y_ + xl_) * 2 + core_}

    t_slot = slot_of(row, slot)
    t_to = {"row": slot, "col": t_slot * 2 + core}
    own = jnp.logical_and(slot == row, t_slot == slot)
    t_from = 0
    for a in range(8):
        t_from = t_from + jnp.where(slot_of(jnp.int32(a), row) == slot, a, 0)
    side = at(row, y, 1 - xl, core)
    above, below = at(row, up, xl, core), at(row, down, xl, core)
    twin = at(row, y, xl, 1 - core)
    zabove, zbelow = at(4 * xh + zup, y, xl, core), at(4 * xh + zdown, y, xl, core)
    across = at(4 * (1 - xh) + z, y, xl, core)

    pieces = coup.shape[0] // PIECE

    def piece_copy(q):
        rows = pl.ds(pl.multiple_of(q * PIECE, PIECE), PIECE)
        return pltpu.make_async_copy(coup.at[rows], stage.at[q % 2], stage_sem.at[q % 2])

    piece_copy(0).start()
    piece_copy(1).start()

    barrier = pltpu.get_barrier_semaphore()
    for other in (side, above, below, twin, zabove, zbelow, across):
        pl.semaphore_signal(barrier, inc=1, device_id=other, device_id_type=MESH)

    @pl.when(jnp.logical_not(own))
    def _():
        pl.semaphore_signal(
            barrier, inc=1, device_id={"row": t_from, "col": row * 2 + core}, device_id_type=MESH
        )
        pl.semaphore_wait(barrier, 8)

    @pl.when(own)
    def _():
        pl.semaphore_wait(barrier, 7)

    def remote(kind, i, src, dst, to):
        return pltpu.make_async_remote_copy(
            src_ref=src,
            dst_ref=dst,
            send_sem=send.at[kind, i],
            recv_sem=recv.at[kind, i],
            device_id=to,
            device_id_type=MESH,
        )

    def rows_of(i, a):
        return p.at[i, pl.ds(pl.multiple_of(a * m, m), m)]

    def t_src(i):
        return pos.at[pl.ds(pl.multiple_of(i * m, m), m)]

    def t_copy(i):
        return remote(T, i, t_src(i), xg.at[i, core, t_slot], t_to)

    def t_local(i):
        return pltpu.make_async_copy(t_src(i), xg.at[i, core, slot], recv.at[T, i])

    def gather_copy(kind, i, slot_, to):
        block = xg.at[i, core, slot_]
        return remote(kind, i, block, block, to)

    def gather_copies(i):
        return {
            XL: lambda: gather_copy(XL, i, slot, side),
            UP: lambda: gather_copy(UP, i, slot, above),
            DN: lambda: gather_copy(DN, i, slot, below),
            UP2: lambda: gather_copy(UP2, i, 2 * y + 1 - xl, above),
            DN2: lambda: gather_copy(DN2, i, 2 * y + 1 - xl, below),
            UPR: lambda: gather_copy(UPR, i, 2 * down + xl, above),
            DNR: lambda: gather_copy(DNR, i, 2 * up + 1 - xl, below),
            SWAP: lambda: remote(SWAP, i, xg.at[i, core], xg.at[i, core], twin),
        }

    def sum_copies(i):
        return {
            ZP: lambda: remote(ZP, i, rows_of(i, zfar), rzp.at[i], zabove),
            ZM: lambda: remote(ZM, i, rows_of(i, 4 + zfar), rzm.at[i], zbelow),
            FP0: lambda: remote(FP0, i, rows_of(i, zup), rfp.at[i, 0], zabove),
            FP1: lambda: remote(FP1, i, rows_of(i, 4 + zup), rfp.at[i, 1], zabove),
            FM0: lambda: remote(FM0, i, rows_of(i, zdown), rfm.at[i, 0], zbelow),
            FM1: lambda: remote(FM1, i, rows_of(i, 4 + zdown), rfm.at[i, 1], zbelow),
            XH: lambda: remote(XH, i, rows_of(i, 4 * (1 - xh) + z), rx.at[i], across),
        }

    def t_start(i):
        @pl.when(own)
        def _():
            t_local(i).start()

        @pl.when(jnp.logical_not(own))
        def _():
            t_copy(i).start()

    def stage_a(i):
        @pl.when(own)
        def _():
            t_local(i).wait()

        @pl.when(jnp.logical_not(own))
        def _():
            t_copy(i).wait_recv()

        c = gather_copies(i)
        for kind in (XL, UP, DN):
            c[kind]().start()

    def stage_b(i):
        c = gather_copies(i)
        c[XL]().wait_recv()
        c[UP2]().start()
        c[DN2]().start()
        c[UP]().wait_recv()
        c[UPR]().start()

    def stage_c(i):
        c = gather_copies(i)
        c[DN2]().wait_recv()
        c[DNR]().start()

    def stage_d(i):
        c = gather_copies(i)
        for kind in (DN, UP2, UPR, DNR):
            c[kind]().wait_recv()
        c[SWAP]().start()

    def convert(q):
        piece_copy(q).wait()
        v = stage[q % 2]
        hi = v.astype(BF16)
        rows = pl.ds(pl.multiple_of(q * PIECE, PIECE), PIECE)
        jhi[rows] = hi
        jlo[rows] = (v - hi.astype(F32)).astype(BF16)

        @pl.when(q + 2 < pieces)
        def _():
            piece_copy(q + 2).start()

    def stage_e(i):
        gather_copies(i)[SWAP]().wait_recv()
        for a in range(8):
            s = slot_of(jnp.int32(a), row)
            for half in range(2):
                v = xg[i, half, s]
                hi = v.astype(BF16)
                columns = slice(half * width, (half + 1) * width)
                x2[a * m : (a + 1) * m, columns] = hi
                x2[(8 + a) * m : (9 + a) * m, columns] = (v - hi.astype(F32)).astype(BF16)

        def tile(t, _):
            c = pl.ds(pl.multiple_of(t * TILE, TILE), TILE)
            both = jnp.dot(x2[...], jhi[:, c], preferred_element_type=F32)
            small = jnp.dot(x2[0 : 8 * m], jlo[:, c], preferred_element_type=F32)
            p[i, :, c] = both[: 8 * m] + (both[8 * m :] + small)
            return 0

        lax.fori_loop(0, width // TILE, tile, 0)
        c = sum_copies(i)
        for kind in (ZP, ZM, FP1, FM0):
            c[kind]().start()

    def stage_g(i):
        c = sum_copies(i)
        for kind, arrived, a, final in ((ZP, rzp, zup, FP0), (ZM, rzm, 4 + zdown, FM1)):
            c[kind]().wait_recv()
            block = rows_of(i, a)
            block[...] = block[...] + arrived[i]
            c[final]().start()

    def stage_h(i):
        c = sum_copies(i)
        for kind in (FP0, FP1, FM0, FM1):
            c[kind]().wait_recv()
        rest = 1 - xh
        block = rows_of(i, 4 * rest + z)
        block[...] = block[...] + (rfp[i, rest] + rfm[i, rest])
        c[XH]().start()
        mine = rows_of(i, 4 * xh + z)
        mine[...] = mine[...] + (rfp[i, xh] + rfm[i, xh])

    def stage_i(i):
        sum_copies(i)[XH]().wait_recv()
        out[pl.ds(pl.multiple_of(i * m, m), m)] = rows_of(i, 4 * xh + z)[...] + rx[i]

    t_start(0)
    t_start(1)
    per = pieces // 4

    def step(t, _):
        @pl.when(t + 2 < n)
        def _():
            t_start(t + 2)

        for stage_, off in (
            (stage_a, 0),
            (stage_b, 1),
            (stage_c, 2),
            (stage_d, 3),
            (stage_g, 5),
            (stage_h, 6),
            (stage_i, 7),
        ):
            i = t - off

            @pl.when(jnp.logical_and(i >= 0, i < n))
            def _():
                stage_(i)

        @pl.when(t < 4)
        def _():
            lax.fori_loop(0, per, lambda q, _: (convert(t * per + q), 0)[1], 0)

        i = t - 4

        @pl.when(jnp.logical_and(i >= 0, i < n))
        def _():
            stage_e(i)

        return 0

    lax.fori_loop(0, n + 7, step, 0)

    def drain(i, _):
        @pl.when(jnp.logical_not(own))
        def _():
            t_copy(i).wait_send()

        for c in (gather_copies(i), sum_copies(i)):
            for kind in c:
                c[kind]().wait_send()
        return 0

    lax.fori_loop(0, n, drain, 0)


def coupled_sum(positions, couplings):
    replicas, width = positions.shape
    m = replicas // CHUNKS
    n = CHUNKS
    depth = couplings.shape[0]
    vmem = pltpu.VMEM
    return pl.pallas_call(
        kernel,
        out_shape=jax.ShapeDtypeStruct((replicas, width), F32),
        in_specs=[pl.BlockSpec(memory_space=vmem), pl.BlockSpec(memory_space=pl.ANY)],
        out_specs=pl.BlockSpec(memory_space=vmem),
        scratch_shapes=[
            vmem((n, 2, 8, m, width), F32),
            vmem((depth, width), BF16),
            vmem((depth, width), BF16),
            vmem((2, PIECE, width), F32),
            vmem((16 * m, depth), BF16),
            vmem((n, 8 * m, width), F32),
            vmem((n, m, width), F32),
            vmem((n, m, width), F32),
            vmem((n, 2, m, width), F32),
            vmem((n, 2, m, width), F32),
            vmem((n, m, width), F32),
            pltpu.SemaphoreType.DMA((16, n)),
            pltpu.SemaphoreType.DMA((16, n)),
            pltpu.SemaphoreType.DMA((2,)),
        ],
        compiler_params=pltpu.CompilerParams(
            collective_id=0, has_side_effects=True, vmem_limit_bytes=66000000
        ),
    )(positions, couplings)


def per_device(positions, momenta, couplings):
    coupled = coupled_sum(positions, couplings)
    radius = positions * positions + momenta * momenta
    momenta_next = momenta + time_step * (
        -(kerr_rate * radius - pump_rate + detuning) * positions + coupling_gain * coupled
    )
    radius_next = positions * positions + momenta_next * momenta_next
    positions_next = (
        positions + time_step * (kerr_rate * radius_next + pump_rate + detuning) * momenta_next
    )
    return (positions_next, momenta_next)


def solution(mesh):
    placed = (P("row", "col"), P("row", "col"), P("row", "col"))
    return jax.shard_map(
        per_device,
        mesh=mesh,
        in_specs=placed,
        out_specs=(P("row", "col"), P("row", "col")),
        check_vma=False,
    )
```

```python
import jax
import jax.numpy as jnp
from jax import lax
from jax.experimental import pallas as pl
from jax.experimental.pallas import tpu as pltpu
from jax.sharding import PartitionSpec as P

time_step = 0.5
kerr_rate = 1.0
pump_rate = 0.6
detuning = 0.4
coupling_gain = 1.5

MESH = pl.DeviceIdType.MESH
BF16 = jnp.bfloat16
F32 = jnp.float32
CHUNKS = 8
PIECE = 384
TILE = 512
AHEAD = 1
OFF_T = 0
OFF_B, OFF_UP, OFF_DOWN, OFF_D, OFF_E, OFF_G, OFF_H, OFF_I = 2, 3, 5, 7, 9, 14, 17, 20
(T, XL, UP, UP2, DN, DN2, UPR, DNR, SWAP, ZP, ZM, FP0, FP1, FM0, FM1, XH) = range(16)


def slot_of(a, b, core):
    xh, z = a // 4, a % 4
    y, xl = b // 2, b % 2
    return 2 * ((z + 2 * xl + xh) % 4) + (xh + y) % 2


def kernel(
    pos, coup, out, xg, jhi, jlo, stage, x2, p, rzp, rzm, rfp, rfm, rx, send, recv, stage_sem
):
    n, _, _, m, width = xg.shape
    row, col = lax.axis_index("row"), lax.axis_index("col")
    xh, z = row // 4, row % 4
    core = col % 2
    slot = col // 2
    y, xl = slot // 2, slot % 2
    up, down = (y + 1) % 4, (y + 3) % 4
    zup, zdown, zfar = (z + 1) % 4, (z + 3) % 4, (z + 2) % 4

    def at(row_, y_, xl_, core_):
        return {"row": row_, "col": (2 * y_ + xl_) * 2 + core_}

    t_slot = slot_of(row, slot, core)
    t_to = {"row": slot, "col": t_slot * 2 + core}
    own = jnp.logical_and(slot == row, t_slot == slot)
    t_from = 0
    for a in range(8):
        t_from = t_from + jnp.where(slot_of(jnp.int32(a), row, core) == slot, a, 0)
    side = at(row, y, 1 - xl, core)
    above, below = at(row, up, xl, core), at(row, down, xl, core)
    twin = at(row, y, xl, 1 - core)
    zabove, zbelow = at(4 * xh + zup, y, xl, core), at(4 * xh + zdown, y, xl, core)
    across = at(4 * (1 - xh) + z, y, xl, core)

    pieces = coup.shape[0] // PIECE

    def piece_copy(q):
        rows = pl.ds(pl.multiple_of(q * PIECE, PIECE), PIECE)
        return pltpu.make_async_copy(coup.at[rows], stage.at[q % 2], stage_sem.at[q % 2])

    piece_copy(0).start()
    piece_copy(1).start()

    barrier = pltpu.get_barrier_semaphore()
    for other in (side, above, below, twin, zabove, zbelow, across):
        pl.semaphore_signal(barrier, inc=1, device_id=other, device_id_type=MESH)

    @pl.when(jnp.logical_not(own))
    def _():
        pl.semaphore_signal(
            barrier, inc=1, device_id={"row": t_from, "col": row * 2 + core}, device_id_type=MESH
        )
        pl.semaphore_wait(barrier, 8)

    @pl.when(own)
    def _():
        pl.semaphore_wait(barrier, 7)

    def remote(kind, i, src, dst, to):
        return pltpu.make_async_remote_copy(
            src_ref=src,
            dst_ref=dst,
            send_sem=send.at[kind, i],
            recv_sem=recv.at[kind, i],
            device_id=to,
            device_id_type=MESH,
        )

    def rows_of(i, a):
        return p.at[i, pl.ds(pl.multiple_of(a * m, m), m)]

    def t_src(i):
        return pos.at[pl.ds(pl.multiple_of(i * m, m), m)]

    def t_copy(i):
        return remote(T, i, t_src(i), xg.at[i, core, t_slot], t_to)

    def t_local(i):
        return pltpu.make_async_copy(t_src(i), xg.at[i, core, slot], recv.at[T, i])

    def gather_copy(kind, i, slot_, to):
        block = xg.at[i, core, slot_]
        return remote(kind, i, block, block, to)

    def gather_copies(i):
        return {
            XL: lambda: gather_copy(XL, i, slot, side),
            UP: lambda: gather_copy(UP, i, slot, above),
            DN: lambda: gather_copy(DN, i, slot, below),
            UP2: lambda: gather_copy(UP2, i, 2 * y + 1 - xl, above),
            DN2: lambda: gather_copy(DN2, i, 2 * y + 1 - xl, below),
            UPR: lambda: gather_copy(UPR, i, 2 * down + xl, above),
            DNR: lambda: gather_copy(DNR, i, 2 * up + 1 - xl, below),
            SWAP: lambda: remote(SWAP, i, xg.at[i, core], xg.at[i, core], twin),
        }

    def sum_copies(i):
        return {
            ZP: lambda: remote(ZP, i, rows_of(i, zfar), rzp.at[i], zabove),
            ZM: lambda: remote(ZM, i, rows_of(i, 4 + zfar), rzm.at[i], zbelow),
            FP0: lambda: remote(FP0, i, rows_of(i, zup), rfp.at[i, 0], zabove),
            FP1: lambda: remote(FP1, i, rows_of(i, 4 + zup), rfp.at[i, 1], zabove),
            FM0: lambda: remote(FM0, i, rows_of(i, zdown), rfm.at[i, 0], zbelow),
            FM1: lambda: remote(FM1, i, rows_of(i, 4 + zdown), rfm.at[i, 1], zbelow),
            XH: lambda: remote(XH, i, rows_of(i, 4 * (1 - xh) + z), rx.at[i], across),
        }

    def t_start(i):
        @pl.when(own)
        def _():
            t_local(i).start()

        @pl.when(jnp.logical_not(own))
        def _():
            t_copy(i).start()

    def t_next(i):
        @pl.when(i + AHEAD < n)
        def _():
            t_start(i + AHEAD)

    def stage_a(i):
        @pl.when(own)
        def _():
            t_local(i).wait()

        @pl.when(jnp.logical_not(own))
        def _():
            t_copy(i).wait_recv()

        c = gather_copies(i)
        for kind in (XL, UP, DN):
            c[kind]().start()

    def stage_b(i):
        c = gather_copies(i)
        c[XL]().wait_recv()
        c[UP2]().start()
        c[DN2]().start()

    def stage_up(i):
        c = gather_copies(i)
        c[UP]().wait_recv()
        c[UPR]().start()

    def stage_down(i):
        c = gather_copies(i)
        c[DN2]().wait_recv()
        c[DNR]().start()

    def stage_d(i):
        c = gather_copies(i)
        for kind in (DN, UP2, UPR, DNR):
            c[kind]().wait_recv()
        c[SWAP]().start()

    def convert(q):
        piece_copy(q).wait()
        v = stage[q % 2]
        hi = v.astype(BF16)
        rows = pl.ds(pl.multiple_of(q * PIECE, PIECE), PIECE)
        jhi[rows] = hi
        jlo[rows] = (v - hi.astype(F32)).astype(BF16)

        @pl.when(q + 2 < pieces)
        def _():
            piece_copy(q + 2).start()

    def stage_split(i):
        gather_copies(i)[SWAP]().wait_recv()
        for a in range(0, 8, 2):
            for half in range(2):
                v = jnp.concatenate(
                    [xg[i, half, slot_of(jnp.int32(a + d), row, half)] for d in range(2)], axis=0
                )
                hi = v.astype(BF16)
                columns = slice(half * width, (half + 1) * width)
                x2[a * m : (a + 2) * m, columns] = hi
                x2[(8 + a) * m : (10 + a) * m, columns] = (v - hi.astype(F32)).astype(BF16)

    def stage_tile(t, i):
        c = pl.ds(pl.multiple_of(t * TILE, TILE), TILE)
        both = jnp.dot(x2[...], jhi[:, c], preferred_element_type=F32)
        small = jnp.dot(x2[0 : 8 * m], jlo[:, c], preferred_element_type=F32)
        p[i, :, c] = both[: 8 * m] + (both[8 * m :] + small)

    def stage_f(i):
        c = sum_copies(i)
        for kind in (ZP, ZM, FP1, FM0):
            c[kind]().start()

    def stage_g(i):
        c = sum_copies(i)
        for kind, arrived, a, final in ((ZP, rzp, zup, FP0), (ZM, rzm, 4 + zdown, FM1)):
            c[kind]().wait_recv()
            block = rows_of(i, a)
            block[...] = block[...] + arrived[i]
            c[final]().start()

    def stage_h(i):
        c = sum_copies(i)
        for kind in (FP0, FP1, FM0, FM1):
            c[kind]().wait_recv()
        rest = 1 - xh
        block = rows_of(i, 4 * rest + z)
        block[...] = block[...] + (rfp[i, rest] + rfm[i, rest])
        c[XH]().start()
        mine = rows_of(i, 4 * xh + z)
        mine[...] = mine[...] + (rfp[i, xh] + rfm[i, xh])

    def stage_i(i):
        sum_copies(i)[XH]().wait_recv()
        out[pl.ds(pl.multiple_of(i * m, m), m)] = rows_of(i, 4 * xh + z)[...] + rx[i]

    stages = (
        (OFF_T, t_next),
        (0, stage_a),
        (OFF_B, stage_b),
        (OFF_UP, stage_up),
        (OFF_DOWN, stage_down),
        (OFF_D, stage_d),
        (OFF_E + 3, stage_f),
        (OFF_G, stage_g),
        (OFF_H, stage_h),
        (OFF_I, stage_i),
        (OFF_E, stage_split),
    )
    last = max(off for off, _ in stages)
    for i in range(AHEAD):
        t_start(i)

    def step(u, _):
        for off, stage_ in stages:
            i = (u - off) // 3

            @pl.when(jnp.logical_and(u >= off, jnp.logical_and(i < n, (u - off) % 3 == 0)))
            def _():
                stage_(i)

        i = (u - OFF_E) // 3

        @pl.when(jnp.logical_and(u >= OFF_E, i < n))
        def _():
            stage_tile((u - OFF_E) % 3, i)

        @pl.when(u < pieces)
        def _():
            convert(u)

        return 0

    lax.fori_loop(0, 3 * (n - 1) + last + 1, step, 0)

    def drain(i, _):
        @pl.when(jnp.logical_not(own))
        def _():
            t_copy(i).wait_send()

        for c in (gather_copies(i), sum_copies(i)):
            for kind in c:
                c[kind]().wait_send()
        return 0

    lax.fori_loop(0, n, drain, 0)


def coupled_sum(positions, couplings):
    replicas, width = positions.shape
    m = replicas // CHUNKS
    n = CHUNKS
    depth = couplings.shape[0]
    vmem = pltpu.VMEM
    return pl.pallas_call(
        kernel,
        out_shape=jax.ShapeDtypeStruct((replicas, width), F32),
        in_specs=[pl.BlockSpec(memory_space=vmem), pl.BlockSpec(memory_space=pl.ANY)],
        out_specs=pl.BlockSpec(memory_space=vmem),
        scratch_shapes=[
            vmem((n, 2, 8, m, width), F32),
            vmem((depth, width), BF16),
            vmem((depth, width), BF16),
            vmem((2, PIECE, width), F32),
            vmem((16 * m, depth), BF16),
            vmem((n, 8 * m, width), F32),
            vmem((n, m, width), F32),
            vmem((n, m, width), F32),
            vmem((n, 2, m, width), F32),
            vmem((n, 2, m, width), F32),
            vmem((n, m, width), F32),
            pltpu.SemaphoreType.DMA((16, n)),
            pltpu.SemaphoreType.DMA((16, n)),
            pltpu.SemaphoreType.DMA((2,)),
        ],
        compiler_params=pltpu.CompilerParams(
            collective_id=0, has_side_effects=True, vmem_limit_bytes=66000000
        ),
    )(positions, couplings)


def per_device(positions, momenta, couplings):
    coupled = coupled_sum(positions, couplings)
    radius = positions * positions + momenta * momenta
    momenta_next = momenta + time_step * (
        -(kerr_rate * radius - pump_rate + detuning) * positions + coupling_gain * coupled
    )
    radius_next = positions * positions + momenta_next * momenta_next
    positions_next = (
        positions + time_step * (kerr_rate * radius_next + pump_rate + detuning) * momenta_next
    )
    return (positions_next, momenta_next)


def solution(mesh):
    placed = (P("row", "col"), P("row", "col"), P("row", "col"))
    return jax.shard_map(
        per_device,
        mesh=mesh,
        in_specs=placed,
        out_specs=(P("row", "col"), P("row", "col")),
        check_vma=False,
    )
```

```python
import jax
import jax.numpy as jnp
from jax import lax
from jax.experimental import pallas as pl
from jax.experimental.pallas import tpu as pltpu
from jax.sharding import PartitionSpec as P

time_step = 0.5
kerr_rate = 1.0
pump_rate = 0.6
detuning = 0.4
coupling_gain = 1.5

MESH = pl.DeviceIdType.MESH
BF16 = jnp.bfloat16
F32 = jnp.float32
CHUNKS = 8
PIECE = 384
TILE = 512
AHEAD = 3
OFF_T = 0
OFF_B, OFF_UP, OFF_DOWN, OFF_D, OFF_E, OFF_G, OFF_H, OFF_I = 3, 3, 6, 9, 11, 16, 19, 22
(T, XL, UP, UP2, DN, DN2, UPR, DNR, SWAP, ZP, ZM, FP0, FP1, FM0, FM1, XH, T1, XL2) = range(18)


def slot_of(a, b, core):
    xh, z = a // 4, a % 4
    y, xl = b // 2, b % 2
    return 2 * ((2 * core + z + 4 - y + xh) % 4) + (xh + y + xl) % 2


def kernel(
    pos, coup, out, xg, turned, jhi, jlo, stage, x2, p, rzp, rzm, rfp, rfm, rx, send, recv, stage_sem
):
    n, _, _, m, width = xg.shape
    row, col = lax.axis_index("row"), lax.axis_index("col")
    xh, z = row // 4, row % 4
    core = col % 2
    slot = col // 2
    y, xl = slot // 2, slot % 2
    up, down = (y + 1) % 4, (y + 3) % 4
    zup, zdown, zfar = (z + 1) % 4, (z + 3) % 4, (z + 2) % 4

    def at(row_, y_, xl_, core_):
        return {"row": row_, "col": (2 * y_ + xl_) * 2 + core_}

    turn = (2 * core + z + 4 - y + xh) % 4
    turn_to = at(row, turn, xl, core)
    stays = turn == y
    t_block = 2 * turn + xl
    t_slot = slot_of(row, t_block, core)
    t_to = {"row": t_block, "col": t_slot * 2 + core}
    own = jnp.logical_and(t_block == row, t_slot == slot)
    t_from = 0
    for a in range(8):
        t_from = t_from + jnp.where(slot_of(jnp.int32(a), row, core) == slot, a, 0)
    beyond = at(row, (y + 2) % 4, xl, core)
    side = at(row, y, 1 - xl, core)
    above, below = at(row, up, xl, core), at(row, down, xl, core)
    twin = at(row, y, xl, 1 - core)
    zabove, zbelow = at(4 * xh + zup, y, xl, core), at(4 * xh + zdown, y, xl, core)
    across = at(4 * (1 - xh) + z, y, xl, core)

    pieces = coup.shape[0] // PIECE

    def piece_copy(q):
        rows = pl.ds(pl.multiple_of(q * PIECE, PIECE), PIECE)
        return pltpu.make_async_copy(coup.at[rows], stage.at[q % 2], stage_sem.at[q % 2])

    piece_copy(0).start()
    piece_copy(1).start()

    barrier = pltpu.get_barrier_semaphore()
    for other in (side, above, below, beyond, twin, zabove, zbelow, across):
        pl.semaphore_signal(barrier, inc=1, device_id=other, device_id_type=MESH)

    @pl.when(jnp.logical_not(own))
    def _():
        pl.semaphore_signal(
            barrier, inc=1, device_id=at(t_from, y, row % 2, core), device_id_type=MESH
        )
        pl.semaphore_wait(barrier, 9)

    @pl.when(own)
    def _():
        pl.semaphore_wait(barrier, 8)

    def remote(kind, i, src, dst, to):
        return pltpu.make_async_remote_copy(
            src_ref=src,
            dst_ref=dst,
            send_sem=send.at[kind, i],
            recv_sem=recv.at[kind, i],
            device_id=to,
            device_id_type=MESH,
        )

    def rows_of(i, a):
        return p.at[i, pl.ds(pl.multiple_of(a * m, m), m)]

    def t_src(i):
        return pos.at[pl.ds(pl.multiple_of(i * m, m), m)]

    def turn_copy(i):
        return remote(T1, i, t_src(i), turned.at[i], turn_to)

    def turn_local(i):
        return pltpu.make_async_copy(t_src(i), turned.at[i], recv.at[T1, i])

    def t_copy(i):
        return remote(T, i, turned.at[i], xg.at[i, core, t_slot], t_to)

    def t_local(i):
        return pltpu.make_async_copy(turned.at[i], xg.at[i, core, slot], recv.at[T, i])

    def gather_copy(kind, i, slot_, to):
        block = xg.at[i, core, slot_]
        return remote(kind, i, block, block, to)

    def half_copy(kind, i, slot_, half, to):
        block = xg.at[i, core, slot_, pl.ds(half * (m // 2), m // 2)]
        return remote(kind, i, block, block, to)

    def gather_copies(i):
        return {
            XL: lambda: gather_copy(XL, i, slot, side),
            UP: lambda: gather_copy(UP, i, slot, above),
            DN: lambda: gather_copy(DN, i, slot, below),
            UP2: lambda: gather_copy(UP2, i, 2 * y + 1 - xl, above),
            DN2: lambda: gather_copy(DN2, i, 2 * y + 1 - xl, below),
            UPR: lambda: half_copy(UPR, i, 2 * down + xl, 0, above),
            DNR: lambda: half_copy(DNR, i, 2 * up + xl, 1, below),
            XL2: lambda: gather_copy(XL2, i, 2 * ((y + 2) % 4) + xl, side),
            SWAP: lambda: remote(SWAP, i, xg.at[i, core], xg.at[i, core], twin),
        }

    def sum_copies(i):
        return {
            ZP: lambda: remote(ZP, i, rows_of(i, zfar), rzp.at[i], zabove),
            ZM: lambda: remote(ZM, i, rows_of(i, 4 + zfar), rzm.at[i], zbelow),
            FP0: lambda: remote(FP0, i, rows_of(i, zup), rfp.at[i, 0], zabove),
            FP1: lambda: remote(FP1, i, rows_of(i, 4 + zup), rfp.at[i, 1], zabove),
            FM0: lambda: remote(FM0, i, rows_of(i, zdown), rfm.at[i, 0], zbelow),
            FM1: lambda: remote(FM1, i, rows_of(i, 4 + zdown), rfm.at[i, 1], zbelow),
            XH: lambda: remote(XH, i, rows_of(i, 4 * (1 - xh) + z), rx.at[i], across),
        }

    def turn_start(i):
        @pl.when(stays)
        def _():
            turn_local(i).start()

        @pl.when(jnp.logical_not(stays))
        def _():
            turn_copy(i).start()

    def t_start(i):
        @pl.when(stays)
        def _():
            turn_local(i).wait()

        @pl.when(jnp.logical_not(stays))
        def _():
            turn_copy(i).wait_recv()

        @pl.when(own)
        def _():
            t_local(i).start()

        @pl.when(jnp.logical_not(own))
        def _():
            t_copy(i).start()

    def turn_next(i):
        @pl.when(i + AHEAD + 1 < n)
        def _():
            turn_start(i + AHEAD + 1)

    def t_next(i):
        @pl.when(i + AHEAD < n)
        def _():
            t_start(i + AHEAD)

    def stage_a(i):
        @pl.when(own)
        def _():
            t_local(i).wait()

        @pl.when(jnp.logical_not(own))
        def _():
            t_copy(i).wait_recv()

        c = gather_copies(i)
        for kind in (XL, UP, DN):
            c[kind]().start()

    def stage_b(i):
        c = gather_copies(i)
        c[XL]().wait_recv()
        c[UP2]().start()
        c[DN2]().start()

    def stage_up(i):
        c = gather_copies(i)
        c[UP]().wait_recv()
        c[UPR]().start()
        c[DN]().wait_recv()
        c[DNR]().start()

    def stage_down(i):
        c = gather_copies(i)
        c[UPR]().wait_recv()
        c[DNR]().wait_recv()
        c[XL2]().start()

    def stage_d(i):
        c = gather_copies(i)
        for kind in (UP2, DN2, XL2):
            c[kind]().wait_recv()
        c[SWAP]().start()

    def convert(q):
        piece_copy(q).wait()
        v = stage[q % 2]
        hi = v.astype(BF16)
        rows = pl.ds(pl.multiple_of(q * PIECE, PIECE), PIECE)
        jhi[rows] = hi
        jlo[rows] = (v - hi.astype(F32)).astype(BF16)

        @pl.when(q + 2 < pieces)
        def _():
            piece_copy(q + 2).start()

    def stage_split(i):
        gather_copies(i)[SWAP]().wait_recv()
        for a in range(0, 8, 2):
            for half in range(2):
                v = jnp.concatenate(
                    [xg[i, half, slot_of(jnp.int32(a + d), row, half)] for d in range(2)], axis=0
                )
                hi = v.astype(BF16)
                columns = slice(half * width, (half + 1) * width)
                x2[a * m : (a + 2) * m, columns] = hi
                x2[(8 + a) * m : (10 + a) * m, columns] = (v - hi.astype(F32)).astype(BF16)

    def stage_tile(t, i):
        c = pl.ds(pl.multiple_of(t * TILE, TILE), TILE)
        both = jnp.dot(x2[...], jhi[:, c], preferred_element_type=F32)
        small = jnp.dot(x2[0 : 8 * m], jlo[:, c], preferred_element_type=F32)
        p[i, :, c] = both[: 8 * m] + (both[8 * m :] + small)

    def stage_f(i):
        c = sum_copies(i)
        for kind in (ZP, ZM, FP1, FM0):
            c[kind]().start()

    def stage_g(i):
        c = sum_copies(i)
        for kind, arrived, a, final in ((ZP, rzp, zup, FP0), (ZM, rzm, 4 + zdown, FM1)):
            c[kind]().wait_recv()
            block = rows_of(i, a)
            block[...] = block[...] + arrived[i]
            c[final]().start()

    def stage_h(i):
        c = sum_copies(i)
        for kind in (FP0, FP1, FM0, FM1):
            c[kind]().wait_recv()
        rest = 1 - xh
        block = rows_of(i, 4 * rest + z)
        block[...] = block[...] + (rfp[i, rest] + rfm[i, rest])
        c[XH]().start()
        mine = rows_of(i, 4 * xh + z)
        mine[...] = mine[...] + (rfp[i, xh] + rfm[i, xh])

    def stage_i(i):
        sum_copies(i)[XH]().wait_recv()
        out[pl.ds(pl.multiple_of(i * m, m), m)] = rows_of(i, 4 * xh + z)[...] + rx[i]

    stages = (
        (0, turn_next),
        (0, stage_a),
        (OFF_T, t_next),
        (OFF_B, stage_b),
        (OFF_UP, stage_up),
        (OFF_DOWN, stage_down),
        (OFF_D, stage_d),
        (OFF_E + 3, stage_f),
        (OFF_G, stage_g),
        (OFF_H, stage_h),
        (OFF_I, stage_i),
        (OFF_E, stage_split),
    )
    last = max(off for off, _ in stages)
    for i in range(AHEAD + 1):
        turn_start(i)
    for i in range(AHEAD):
        t_start(i)

    def step(u, _):
        for off, stage_ in stages:
            i = (u - off) // 3

            @pl.when(jnp.logical_and(u >= off, jnp.logical_and(i < n, (u - off) % 3 == 0)))
            def _():
                stage_(i)

        i = (u - OFF_E) // 3

        @pl.when(jnp.logical_and(u >= OFF_E, i < n))
        def _():
            stage_tile((u - OFF_E) % 3, i)

        @pl.when(u < pieces)
        def _():
            convert(u)

        return 0

    lax.fori_loop(0, 3 * (n - 1) + last + 1, step, 0)

    def drain(i, _):
        @pl.when(jnp.logical_not(own))
        def _():
            t_copy(i).wait_send()

        @pl.when(jnp.logical_not(stays))
        def _():
            turn_copy(i).wait_send()

        for c in (gather_copies(i), sum_copies(i)):
            for kind in c:
                c[kind]().wait_send()
        return 0

    lax.fori_loop(0, n, drain, 0)


def coupled_sum(positions, couplings):
    replicas, width = positions.shape
    m = replicas // CHUNKS
    n = CHUNKS
    depth = couplings.shape[0]
    vmem = pltpu.VMEM
    return pl.pallas_call(
        kernel,
        out_shape=jax.ShapeDtypeStruct((replicas, width), F32),
        in_specs=[pl.BlockSpec(memory_space=vmem), pl.BlockSpec(memory_space=pl.ANY)],
        out_specs=pl.BlockSpec(memory_space=vmem),
        scratch_shapes=[
            vmem((n, 2, 8, m, width), F32),
            vmem((n, m, width), F32),
            vmem((depth, width), BF16),
            vmem((depth, width), BF16),
            vmem((2, PIECE, width), F32),
            vmem((16 * m, depth), BF16),
            vmem((n, 8 * m, width), F32),
            vmem((n, m, width), F32),
            vmem((n, m, width), F32),
            vmem((n, 2, m, width), F32),
            vmem((n, 2, m, width), F32),
            vmem((n, m, width), F32),
            pltpu.SemaphoreType.DMA((18, n)),
            pltpu.SemaphoreType.DMA((18, n)),
            pltpu.SemaphoreType.DMA((2,)),
        ],
        compiler_params=pltpu.CompilerParams(
            collective_id=0, has_side_effects=True, vmem_limit_bytes=66000000
        ),
    )(positions, couplings)


def per_device(positions, momenta, couplings):
    coupled = coupled_sum(positions, couplings)
    radius = positions * positions + momenta * momenta
    momenta_next = momenta + time_step * (
        -(kerr_rate * radius - pump_rate + detuning) * positions + coupling_gain * coupled
    )
    radius_next = positions * positions + momenta_next * momenta_next
    positions_next = (
        positions + time_step * (kerr_rate * radius_next + pump_rate + detuning) * momenta_next
    )
    return (positions_next, momenta_next)


def solution(mesh):
    placed = (P("row", "col"), P("row", "col"), P("row", "col"))
    return jax.shard_map(
        per_device,
        mesh=mesh,
        in_specs=placed,
        out_specs=(P("row", "col"), P("row", "col")),
        check_vma=False,
    )
```

```python
import jax
import jax.numpy as jnp
from jax import lax
from jax.experimental import pallas as pl
from jax.experimental.pallas import tpu as pltpu
from jax.sharding import PartitionSpec as P

time_step = 0.5
kerr_rate = 1.0
pump_rate = 0.6
detuning = 0.4
coupling_gain = 1.5

MESH = pl.DeviceIdType.MESH
BF16 = jnp.bfloat16
F32 = jnp.float32
CHUNKS = 8
PIECE = 384
TILE = 512
AHEAD = 3
OFF_T = 0
OFF_B, OFF_UP, OFF_DOWN, OFF_D, OFF_E, OFF_G, OFF_H, OFF_I = 3, 3, 6, 9, 11, 18, 22, 26
(T, XL, UP, UP2, DN, DN2, UPR, DNR, SWAP, ZP, ZM, FP0, FP1, FM0, FM1, XH, T1, XL2) = range(18)


def slot_of(a, b, core):
    xh, z = a // 4, a % 4
    y, xl = b // 2, b % 2
    return 2 * ((2 * core + z + 4 - y + xh) % 4) + (xh + y + xl) % 2


def kernel(
    pos, coup, out, xg, turned, jhi, jlo, stage, x2, p, rzp, rzm, rfp, rfm, rx, send, recv, stage_sem
):
    n, _, _, m, width = xg.shape
    row, col = lax.axis_index("row"), lax.axis_index("col")
    xh, z = row // 4, row % 4
    core = col % 2
    slot = col // 2
    y, xl = slot // 2, slot % 2
    up, down = (y + 1) % 4, (y + 3) % 4
    zup, zdown, zfar = (z + 1) % 4, (z + 3) % 4, (z + 2) % 4

    def at(row_, y_, xl_, core_):
        return {"row": row_, "col": (2 * y_ + xl_) * 2 + core_}

    turn = (2 * core + z + 4 - y + xh) % 4
    turn_to = at(row, turn, xl, core)
    stays = turn == y
    t_block = 2 * turn + xl
    t_slot = slot_of(row, t_block, core)
    t_to = {"row": t_block, "col": t_slot * 2 + core}
    own = jnp.logical_and(t_block == row, t_slot == slot)
    t_from = 0
    for a in range(8):
        t_from = t_from + jnp.where(slot_of(jnp.int32(a), row, core) == slot, a, 0)
    beyond = at(row, (y + 2) % 4, xl, core)
    side = at(row, y, 1 - xl, core)
    above, below = at(row, up, xl, core), at(row, down, xl, core)
    twin = at(row, y, xl, 1 - core)
    zabove, zbelow = at(4 * xh + zup, y, xl, core), at(4 * xh + zdown, y, xl, core)
    across = at(4 * (1 - xh) + z, y, xl, core)

    pieces = coup.shape[0] // PIECE

    def piece_copy(q):
        rows = pl.ds(pl.multiple_of(q * PIECE, PIECE), PIECE)
        return pltpu.make_async_copy(coup.at[rows], stage.at[q % 2], stage_sem.at[q % 2])

    piece_copy(0).start()
    piece_copy(1).start()

    barrier = pltpu.get_barrier_semaphore()
    for other in (side, above, below, beyond, twin, zabove, zbelow, across):
        pl.semaphore_signal(barrier, inc=1, device_id=other, device_id_type=MESH)

    @pl.when(jnp.logical_not(own))
    def _():
        pl.semaphore_signal(
            barrier, inc=1, device_id=at(t_from, y, row % 2, core), device_id_type=MESH
        )
        pl.semaphore_wait(barrier, 9)

    @pl.when(own)
    def _():
        pl.semaphore_wait(barrier, 8)

    def remote(kind, i, src, dst, to):
        return pltpu.make_async_remote_copy(
            src_ref=src,
            dst_ref=dst,
            send_sem=send.at[kind, i],
            recv_sem=recv.at[kind, i],
            device_id=to,
            device_id_type=MESH,
        )

    def rows_of(i, a):
        return p.at[i, pl.ds(pl.multiple_of(a * m, m), m)]

    def t_src(i):
        return pos.at[pl.ds(pl.multiple_of(i * m, m), m)]

    def turn_copy(i):
        return remote(T1, i, t_src(i), turned.at[i], turn_to)

    def turn_local(i):
        return pltpu.make_async_copy(t_src(i), turned.at[i], recv.at[T1, i])

    def t_copy(i):
        return remote(T, i, turned.at[i], xg.at[i, core, t_slot], t_to)

    def t_local(i):
        return pltpu.make_async_copy(turned.at[i], xg.at[i, core, slot], recv.at[T, i])

    def gather_copy(kind, i, slot_, to):
        block = xg.at[i, core, slot_]
        return remote(kind, i, block, block, to)

    def half_copy(kind, i, slot_, half, to):
        block = xg.at[i, core, slot_, pl.ds(half * (m // 2), m // 2)]
        return remote(kind, i, block, block, to)

    def gather_copies(i):
        return {
            XL: lambda: gather_copy(XL, i, slot, side),
            UP: lambda: gather_copy(UP, i, slot, above),
            DN: lambda: gather_copy(DN, i, slot, below),
            UP2: lambda: gather_copy(UP2, i, 2 * y + 1 - xl, above),
            DN2: lambda: gather_copy(DN2, i, 2 * y + 1 - xl, below),
            UPR: lambda: half_copy(UPR, i, 2 * down + xl, 0, above),
            DNR: lambda: half_copy(DNR, i, 2 * up + xl, 1, below),
            XL2: lambda: gather_copy(XL2, i, 2 * ((y + 2) % 4) + xl, side),
            SWAP: lambda: remote(SWAP, i, xg.at[i, core], xg.at[i, core], twin),
        }

    def sum_copies(i):
        return {
            FP0: lambda: remote(FP0, i, rows_of(i, zup), rfp.at[i, 0], zabove),
            FP1: lambda: remote(FP1, i, rows_of(i, 4 + zup), rfp.at[i, 1], zabove),
            FM0: lambda: remote(FM0, i, rows_of(i, zdown), rfm.at[i, 0], zbelow),
            FM1: lambda: remote(FM1, i, rows_of(i, 4 + zdown), rfm.at[i, 1], zbelow),
            XH: lambda: remote(XH, i, rows_of(i, 4 * (1 - xh) + z), rx.at[i], across),
        }

    def far_copies(t, i):
        c = pl.ds(pl.multiple_of(t * TILE, TILE), TILE)
        return (
            remote(18 + t, i, rows_of(i, zfar).at[:, c], rzp.at[i, :, c], zabove),
            remote(21 + t, i, rows_of(i, 4 + zfar).at[:, c], rzm.at[i, :, c], zbelow),
        )

    def turn_start(i):
        @pl.when(stays)
        def _():
            turn_local(i).start()

        @pl.when(jnp.logical_not(stays))
        def _():
            turn_copy(i).start()

    def t_start(i):
        @pl.when(stays)
        def _():
            turn_local(i).wait()

        @pl.when(jnp.logical_not(stays))
        def _():
            turn_copy(i).wait_recv()

        @pl.when(own)
        def _():
            t_local(i).start()

        @pl.when(jnp.logical_not(own))
        def _():
            t_copy(i).start()

    def turn_next(i):
        @pl.when(i + AHEAD + 1 < n)
        def _():
            turn_start(i + AHEAD + 1)

    def t_next(i):
        @pl.when(i + AHEAD < n)
        def _():
            t_start(i + AHEAD)

    def stage_a(i):
        @pl.when(own)
        def _():
            t_local(i).wait()

        @pl.when(jnp.logical_not(own))
        def _():
            t_copy(i).wait_recv()

        c = gather_copies(i)
        for kind in (XL, UP, DN):
            c[kind]().start()

    def stage_b(i):
        c = gather_copies(i)
        c[XL]().wait_recv()
        c[UP2]().start()
        c[DN2]().start()

    def stage_up(i):
        c = gather_copies(i)
        c[UP]().wait_recv()
        c[UPR]().start()
        c[DN]().wait_recv()
        c[DNR]().start()

    def stage_down(i):
        c = gather_copies(i)
        c[UPR]().wait_recv()
        c[DNR]().wait_recv()
        c[XL2]().start()

    def stage_d(i):
        c = gather_copies(i)
        for kind in (UP2, DN2, XL2):
            c[kind]().wait_recv()
        c[SWAP]().start()

    def convert(q):
        piece_copy(q).wait()
        v = stage[q % 2]
        hi = v.astype(BF16)
        rows = pl.ds(pl.multiple_of(q * PIECE, PIECE), PIECE)
        jhi[rows] = hi
        jlo[rows] = (v - hi.astype(F32)).astype(BF16)

        @pl.when(q + 2 < pieces)
        def _():
            piece_copy(q + 2).start()

    def stage_split(i):
        gather_copies(i)[SWAP]().wait_recv()
        for a in range(0, 8, 2):
            for half in range(2):
                v = jnp.concatenate(
                    [xg[i, half, slot_of(jnp.int32(a + d), row, half)] for d in range(2)], axis=0
                )
                hi = v.astype(BF16)
                columns = slice(half * width, (half + 1) * width)
                x2[a * m : (a + 2) * m, columns] = hi
                x2[(8 + a) * m : (10 + a) * m, columns] = (v - hi.astype(F32)).astype(BF16)

    def stage_tile(t, i):
        c = pl.ds(pl.multiple_of(t * TILE, TILE), TILE)
        both = jnp.dot(x2[...], jhi[:, c], preferred_element_type=F32)
        small = jnp.dot(x2[0 : 8 * m], jlo[:, c], preferred_element_type=F32)
        p[i, :, c] = both[: 8 * m] + (both[8 * m :] + small)
        for copy in far_copies(t, i):
            copy.start()

    def stage_f(i):
        c = sum_copies(i)
        for kind in (FP1, FM0):
            c[kind]().start()

    def stage_g(i):
        c = sum_copies(i)
        for side_, arrived, a, final in ((0, rzp, zup, FP0), (1, rzm, 4 + zdown, FM1)):
            for t in range(3):
                far_copies(t, i)[side_].wait_recv()
            block = rows_of(i, a)
            block[...] = block[...] + arrived[i]
            c[final]().start()

    def stage_h(i):
        c = sum_copies(i)
        for kind in (FP0, FP1, FM0, FM1):
            c[kind]().wait_recv()
        rest = 1 - xh
        block = rows_of(i, 4 * rest + z)
        block[...] = block[...] + (rfp[i, rest] + rfm[i, rest])
        c[XH]().start()
        mine = rows_of(i, 4 * xh + z)
        mine[...] = mine[...] + (rfp[i, xh] + rfm[i, xh])

    def stage_i(i):
        sum_copies(i)[XH]().wait_recv()
        out[pl.ds(pl.multiple_of(i * m, m), m)] = rows_of(i, 4 * xh + z)[...] + rx[i]

    stages = (
        (0, turn_next),
        (0, stage_a),
        (OFF_T, t_next),
        (OFF_B, stage_b),
        (OFF_UP, stage_up),
        (OFF_DOWN, stage_down),
        (OFF_D, stage_d),
        (OFF_E + 3, stage_f),
        (OFF_G, stage_g),
        (OFF_H, stage_h),
        (OFF_I, stage_i),
        (OFF_E, stage_split),
    )
    last = max(off for off, _ in stages)
    for i in range(AHEAD + 1):
        turn_start(i)
    for i in range(AHEAD):
        t_start(i)

    def step(u, _):
        for off, stage_ in stages:
            i = (u - off) // 3

            @pl.when(jnp.logical_and(u >= off, jnp.logical_and(i < n, (u - off) % 3 == 0)))
            def _():
                stage_(i)

        i = (u - OFF_E) // 3

        @pl.when(jnp.logical_and(u >= OFF_E, i < n))
        def _():
            stage_tile((u - OFF_E) % 3, i)

        @pl.when(u < pieces)
        def _():
            convert(u)

        return 0

    lax.fori_loop(0, 3 * (n - 1) + last + 1, step, 0)

    def drain(i, _):
        @pl.when(jnp.logical_not(own))
        def _():
            t_copy(i).wait_send()

        @pl.when(jnp.logical_not(stays))
        def _():
            turn_copy(i).wait_send()

        for t in range(3):
            for copy in far_copies(t, i):
                copy.wait_send()
        for c in (gather_copies(i), sum_copies(i)):
            for kind in c:
                c[kind]().wait_send()
        return 0

    lax.fori_loop(0, n, drain, 0)


def coupled_sum(positions, couplings):
    replicas, width = positions.shape
    m = replicas // CHUNKS
    n = CHUNKS
    depth = couplings.shape[0]
    vmem = pltpu.VMEM
    return pl.pallas_call(
        kernel,
        out_shape=jax.ShapeDtypeStruct((replicas, width), F32),
        in_specs=[pl.BlockSpec(memory_space=vmem), pl.BlockSpec(memory_space=pl.ANY)],
        out_specs=pl.BlockSpec(memory_space=vmem),
        scratch_shapes=[
            vmem((n, 2, 8, m, width), F32),
            vmem((n, m, width), F32),
            vmem((depth, width), BF16),
            vmem((depth, width), BF16),
            vmem((2, PIECE, width), F32),
            vmem((16 * m, depth), BF16),
            vmem((n, 8 * m, width), F32),
            vmem((n, m, width), F32),
            vmem((n, m, width), F32),
            vmem((n, 2, m, width), F32),
            vmem((n, 2, m, width), F32),
            vmem((n, m, width), F32),
            pltpu.SemaphoreType.DMA((24, n)),
            pltpu.SemaphoreType.DMA((24, n)),
            pltpu.SemaphoreType.DMA((2,)),
        ],
        compiler_params=pltpu.CompilerParams(
            collective_id=0, has_side_effects=True, vmem_limit_bytes=66000000
        ),
    )(positions, couplings)


def per_device(positions, momenta, couplings):
    coupled = coupled_sum(positions, couplings)
    radius = positions * positions + momenta * momenta
    momenta_next = momenta + time_step * (
        -(kerr_rate * radius - pump_rate + detuning) * positions + coupling_gain * coupled
    )
    radius_next = positions * positions + momenta_next * momenta_next
    positions_next = (
        positions + time_step * (kerr_rate * radius_next + pump_rate + detuning) * momenta_next
    )
    return (positions_next, momenta_next)


def solution(mesh):
    placed = (P("row", "col"), P("row", "col"), P("row", "col"))
    return jax.shard_map(
        per_device,
        mesh=mesh,
        in_specs=placed,
        out_specs=(P("row", "col"), P("row", "col")),
        check_vma=False,
    )
```

```python
import jax
import jax.numpy as jnp
from jax import lax
from jax.experimental import pallas as pl
from jax.experimental.pallas import tpu as pltpu
from jax.sharding import PartitionSpec as P

time_step = 0.5
kerr_rate = 1.0
pump_rate = 0.6
detuning = 0.4
coupling_gain = 1.5

MESH = pl.DeviceIdType.MESH
BF16 = jnp.bfloat16
F32 = jnp.float32
CHUNKS = 8
PIECE = 384
TILE = 512
AHEAD = 3
OFF_T = 0
OFF_B, OFF_UP, OFF_DOWN, OFF_D, OFF_E, OFF_G, OFF_H, OFF_I = 3, 3, 6, 9, 11, 18, 22, 26
(T, XL, UP, UP2, DN, DN2, UPR, DNR, SWAP, ZP, ZM, FP0, FP1, FM0, FM1, XH, T1, XL2) = range(18)


def slot_of(a, b, core):
    xh, z = a // 4, a % 4
    y, xl = b // 2, b % 2
    return 2 * ((2 * core + z + 4 - y + xh) % 4) + (xh + y + xl) % 2


def kernel(
    pos, coup, out, xg, turned, jhi, jlo, stage, x2, p, rzp, rzm, rfp, rfm, rx, send, recv, stage_sem
):
    n, _, _, m, width = xg.shape
    row, col = lax.axis_index("row"), lax.axis_index("col")
    xh, z = row // 4, row % 4
    core = col % 2
    slot = col // 2
    y, xl = slot // 2, slot % 2
    up, down = (y + 1) % 4, (y + 3) % 4
    zup, zdown, zfar = (z + 1) % 4, (z + 3) % 4, (z + 2) % 4

    def at(row_, y_, xl_, core_):
        return {"row": row_, "col": (2 * y_ + xl_) * 2 + core_}

    turn = (2 * core + z + 4 - y + xh) % 4
    turn_to = at(row, turn, xl, core)
    stays = turn == y
    t_block = 2 * turn + xl
    t_slot = slot_of(row, t_block, core)
    t_to = {"row": t_block, "col": t_slot * 2 + core}
    own = jnp.logical_and(t_block == row, t_slot == slot)
    t_from = 0
    for a in range(8):
        t_from = t_from + jnp.where(slot_of(jnp.int32(a), row, core) == slot, a, 0)
    beyond = at(row, (y + 2) % 4, xl, core)
    side = at(row, y, 1 - xl, core)
    above, below = at(row, up, xl, core), at(row, down, xl, core)
    twin = at(row, y, xl, 1 - core)
    zabove, zbelow = at(4 * xh + zup, y, xl, core), at(4 * xh + zdown, y, xl, core)
    across = at(4 * (1 - xh) + z, y, xl, core)

    pieces = coup.shape[0] // PIECE

    def piece_copy(q):
        rows = pl.ds(pl.multiple_of(q * PIECE, PIECE), PIECE)
        return pltpu.make_async_copy(coup.at[rows], stage.at[q % 2], stage_sem.at[q % 2])

    piece_copy(0).start()
    piece_copy(1).start()

    barrier = pltpu.get_barrier_semaphore()
    for other in (side, above, below, beyond, twin, zabove, zbelow, across):
        pl.semaphore_signal(barrier, inc=1, device_id=other, device_id_type=MESH)

    @pl.when(jnp.logical_not(own))
    def _():
        pl.semaphore_signal(
            barrier, inc=1, device_id=at(t_from, y, row % 2, core), device_id_type=MESH
        )
        pl.semaphore_wait(barrier, 9)

    @pl.when(own)
    def _():
        pl.semaphore_wait(barrier, 8)

    def remote(kind, i, src, dst, to):
        return pltpu.make_async_remote_copy(
            src_ref=src,
            dst_ref=dst,
            send_sem=send.at[kind, i],
            recv_sem=recv.at[kind, i],
            device_id=to,
            device_id_type=MESH,
        )

    def rows_of(i, a):
        return p.at[i, pl.ds(pl.multiple_of(a * m, m), m)]

    def t_src(i):
        return pos.at[pl.ds(pl.multiple_of(i * m, m), m)]

    def turn_copy(i):
        return remote(T1, i, t_src(i), turned.at[i], turn_to)

    def turn_local(i):
        return pltpu.make_async_copy(t_src(i), turned.at[i], recv.at[T1, i])

    def t_copy(i):
        return remote(T, i, turned.at[i], xg.at[i, core, t_slot], t_to)

    def t_local(i):
        return pltpu.make_async_copy(turned.at[i], xg.at[i, core, slot], recv.at[T, i])

    def gather_copy(kind, i, slot_, to):
        block = xg.at[i, core, slot_]
        return remote(kind, i, block, block, to)

    def half_copy(kind, i, slot_, half, to):
        block = xg.at[i, core, slot_, pl.ds(half * (m // 2), m // 2)]
        return remote(kind, i, block, block, to)

    def gather_copies(i):
        return {
            XL: lambda: gather_copy(XL, i, slot, side),
            UP: lambda: gather_copy(UP, i, slot, above),
            DN: lambda: gather_copy(DN, i, slot, below),
            UP2: lambda: gather_copy(UP2, i, 2 * y + 1 - xl, above),
            DN2: lambda: gather_copy(DN2, i, 2 * y + 1 - xl, below),
            UPR: lambda: half_copy(UPR, i, 2 * down + xl, 0, above),
            DNR: lambda: half_copy(DNR, i, 2 * up + xl, 1, below),
            XL2: lambda: gather_copy(XL2, i, 2 * ((y + 2) % 4) + xl, side),
            SWAP: lambda: remote(SWAP, i, xg.at[i, core], xg.at[i, core], twin),
        }

    def sum_copies(i):
        return {
            FP0: lambda: remote(FP0, i, rows_of(i, zup), rfp.at[i, 0], zabove),
            FM1: lambda: remote(FM1, i, rows_of(i, 4 + zdown), rfm.at[i, 1], zbelow),
            XH: lambda: remote(XH, i, rows_of(i, 4 * (1 - xh) + z), rx.at[i], across),
        }

    def tile_copies(t, i):
        c = pl.ds(pl.multiple_of(t * TILE, TILE), TILE)
        return (
            remote(18 + t, i, rows_of(i, zfar).at[:, c], rzp.at[i, :, c], zabove),
            remote(21 + t, i, rows_of(i, 4 + zfar).at[:, c], rzm.at[i, :, c], zbelow),
            remote(24 + t, i, rows_of(i, 4 + zup).at[:, c], rfp.at[i, 1, :, c], zabove),
            remote(27 + t, i, rows_of(i, zdown).at[:, c], rfm.at[i, 0, :, c], zbelow),
        )

    def turn_start(i):
        @pl.when(stays)
        def _():
            turn_local(i).start()

        @pl.when(jnp.logical_not(stays))
        def _():
            turn_copy(i).start()

    def t_start(i):
        @pl.when(stays)
        def _():
            turn_local(i).wait()

        @pl.when(jnp.logical_not(stays))
        def _():
            turn_copy(i).wait_recv()

        @pl.when(own)
        def _():
            t_local(i).start()

        @pl.when(jnp.logical_not(own))
        def _():
            t_copy(i).start()

    def turn_next(i):
        @pl.when(i + AHEAD + 1 < n)
        def _():
            turn_start(i + AHEAD + 1)

    def t_next(i):
        @pl.when(i + AHEAD < n)
        def _():
            t_start(i + AHEAD)

    def stage_a(i):
        @pl.when(own)
        def _():
            t_local(i).wait()

        @pl.when(jnp.logical_not(own))
        def _():
            t_copy(i).wait_recv()

        c = gather_copies(i)
        for kind in (XL, UP, DN):
            c[kind]().start()

    def stage_b(i):
        c = gather_copies(i)
        c[XL]().wait_recv()
        c[UP2]().start()
        c[DN2]().start()

    def stage_up(i):
        c = gather_copies(i)
        c[UP]().wait_recv()
        c[UPR]().start()
        c[DN]().wait_recv()
        c[DNR]().start()

    def stage_down(i):
        c = gather_copies(i)
        c[UPR]().wait_recv()
        c[DNR]().wait_recv()
        c[XL2]().start()

    def stage_d(i):
        c = gather_copies(i)
        for kind in (UP2, DN2, XL2):
            c[kind]().wait_recv()
        c[SWAP]().start()

    def convert(q):
        piece_copy(q).wait()
        v = stage[q % 2]
        hi = v.astype(BF16)
        rows = pl.ds(pl.multiple_of(q * PIECE, PIECE), PIECE)
        jhi[rows] = hi
        jlo[rows] = (v - hi.astype(F32)).astype(BF16)

        @pl.when(q + 2 < pieces)
        def _():
            piece_copy(q + 2).start()

    def stage_split(i):
        gather_copies(i)[SWAP]().wait_recv()
        for a in range(0, 8, 2):
            for half in range(2):
                v = jnp.concatenate(
                    [xg[i, half, slot_of(jnp.int32(a + d), row, half)] for d in range(2)], axis=0
                )
                hi = v.astype(BF16)
                columns = slice(half * width, (half + 1) * width)
                x2[a * m : (a + 2) * m, columns] = hi
                x2[(8 + a) * m : (10 + a) * m, columns] = (v - hi.astype(F32)).astype(BF16)

    def stage_tile(t, i):
        c = pl.ds(pl.multiple_of(t * TILE, TILE), TILE)
        both = jnp.dot(x2[...], jhi[:, c], preferred_element_type=F32)
        small = jnp.dot(x2[0 : 8 * m], jlo[:, c], preferred_element_type=F32)
        p[i, :, c] = both[: 8 * m] + (both[8 * m :] + small)
        for copy in tile_copies(t, i):
            copy.start()

    def stage_g(i):
        c = sum_copies(i)
        for side_, arrived, a, final in ((0, rzp, zup, FP0), (1, rzm, 4 + zdown, FM1)):
            for t in range(3):
                tile_copies(t, i)[side_].wait_recv()
            block = rows_of(i, a)
            block[...] = block[...] + arrived[i]
            c[final]().start()

    def stage_h(i):
        c = sum_copies(i)
        for kind in (FP0, FM1):
            c[kind]().wait_recv()
        for t in range(3):
            for copy in tile_copies(t, i)[2:]:
                copy.wait_recv()
        rest = 1 - xh
        block = rows_of(i, 4 * rest + z)
        block[...] = block[...] + (rfp[i, rest] + rfm[i, rest])
        c[XH]().start()
        mine = rows_of(i, 4 * xh + z)
        mine[...] = mine[...] + (rfp[i, xh] + rfm[i, xh])

    def stage_i(i):
        sum_copies(i)[XH]().wait_recv()
        out[pl.ds(pl.multiple_of(i * m, m), m)] = rows_of(i, 4 * xh + z)[...] + rx[i]

    stages = (
        (0, turn_next),
        (0, stage_a),
        (OFF_T, t_next),
        (OFF_B, stage_b),
        (OFF_UP, stage_up),
        (OFF_DOWN, stage_down),
        (OFF_D, stage_d),
        (OFF_G, stage_g),
        (OFF_H, stage_h),
        (OFF_I, stage_i),
        (OFF_E, stage_split),
    )
    last = max(off for off, _ in stages)
    for i in range(AHEAD + 1):
        turn_start(i)
    for i in range(AHEAD):
        t_start(i)

    def step(u, _):
        for off, stage_ in stages:
            i = (u - off) // 3

            @pl.when(jnp.logical_and(u >= off, jnp.logical_and(i < n, (u - off) % 3 == 0)))
            def _():
                stage_(i)

        i = (u - OFF_E) // 3

        @pl.when(jnp.logical_and(u >= OFF_E, i < n))
        def _():
            stage_tile((u - OFF_E) % 3, i)

        @pl.when(u < pieces)
        def _():
            convert(u)

        return 0

    lax.fori_loop(0, 3 * (n - 1) + last + 1, step, 0)

    def drain(i, _):
        @pl.when(jnp.logical_not(own))
        def _():
            t_copy(i).wait_send()

        @pl.when(jnp.logical_not(stays))
        def _():
            turn_copy(i).wait_send()

        for t in range(3):
            for copy in tile_copies(t, i):
                copy.wait_send()
        for c in (gather_copies(i), sum_copies(i)):
            for kind in c:
                c[kind]().wait_send()
        return 0

    lax.fori_loop(0, n, drain, 0)


def coupled_sum(positions, couplings):
    replicas, width = positions.shape
    m = replicas // CHUNKS
    n = CHUNKS
    depth = couplings.shape[0]
    vmem = pltpu.VMEM
    return pl.pallas_call(
        kernel,
        out_shape=jax.ShapeDtypeStruct((replicas, width), F32),
        in_specs=[pl.BlockSpec(memory_space=vmem), pl.BlockSpec(memory_space=pl.ANY)],
        out_specs=pl.BlockSpec(memory_space=vmem),
        scratch_shapes=[
            vmem((n, 2, 8, m, width), F32),
            vmem((n, m, width), F32),
            vmem((depth, width), BF16),
            vmem((depth, width), BF16),
            vmem((2, PIECE, width), F32),
            vmem((16 * m, depth), BF16),
            vmem((n, 8 * m, width), F32),
            vmem((n, m, width), F32),
            vmem((n, m, width), F32),
            vmem((n, 2, m, width), F32),
            vmem((n, 2, m, width), F32),
            vmem((n, m, width), F32),
            pltpu.SemaphoreType.DMA((30, n)),
            pltpu.SemaphoreType.DMA((30, n)),
            pltpu.SemaphoreType.DMA((2,)),
        ],
        compiler_params=pltpu.CompilerParams(
            collective_id=0, has_side_effects=True, vmem_limit_bytes=66000000
        ),
    )(positions, couplings)


def per_device(positions, momenta, couplings):
    coupled = coupled_sum(positions, couplings)
    radius = positions * positions + momenta * momenta
    momenta_next = momenta + time_step * (
        -(kerr_rate * radius - pump_rate + detuning) * positions + coupling_gain * coupled
    )
    radius_next = positions * positions + momenta_next * momenta_next
    positions_next = (
        positions + time_step * (kerr_rate * radius_next + pump_rate + detuning) * momenta_next
    )
    return (positions_next, momenta_next)


def solution(mesh):
    placed = (P("row", "col"), P("row", "col"), P("row", "col"))
    return jax.shard_map(
        per_device,
        mesh=mesh,
        in_specs=placed,
        out_specs=(P("row", "col"), P("row", "col")),
        check_vma=False,
    )
```
